32 devices in a mesh: dir: 2 (over y), row: 4 (over z), col: 4 (over x, core).
Axes of the slice: x: 2, y: 2, z: 4, core: 2. Of those that a mesh axis runs over, the one named last changes fastest.
Arguments:
- cotangent: bfloat16 [2048, 512], P('dir'), may hold values from -3 to 3
- radiation: bfloat16 [2, 8192, 2048], P(None, ('row', 'col'), 'dir'), may hold values from -0.125 to 0.125
- near_z: float32 [2, 256, 512, 512], P(None, ('dir', 'row', 'col')), may hold values from -0.25 to 0.25
- near_pairs: int32 [256, 2], P(('dir', 'row', 'col')), may hold values from 0 to 15, as said below
- far_ut: float32 [2, 128, 96, 512], P(None, ('dir', 'row', 'col')), may hold values from -0.25 to 0.25
- far_vt: float32 [2, 128, 96, 512], P(None, ('dir', 'row', 'col')), may hold values from -0.625 to 0.625
- far_pairs: int32 [128, 2], P(('dir', 'row', 'col')), may hold values from 0 to 15, as said below
- far_ranks: int32 [128], P(('dir', 'row', 'col')), may hold values from 32 to 96
- block_counts: int32 [32, 2], P(('dir', 'row', 'col')), may hold values from 1 to 8, as said below
Outputs:
- adjoint: float32 [8192, 512], P(('col', 'dir', 'row'))
The draws below stay inside these ranges and needn't reach their ends.
Inputs may be any that keep to these rules, and one draw needn't show every extreme that they name: `near_pairs`: slot s belongs to the device at position g = s div 8 in the order dir, row, col, with row index r and column index c; its row cluster lies in r * 4 to (r + 1) * 4 - 1 and its column cluster in c * 4 to (c + 1) * 4 - 1. Pairs may repeat. `far_pairs`: slot s belongs to the device at position s div 4 in the order dir, row, col, with row index r and column index c; its row cluster lies in r * 4 to (r + 1) * 4 - 1 and its column cluster in c * 4 to (c + 1) * 4 - 1. Pairs may repeat. `block_counts`: column 0 is at most 8 and column 1 at most 4; the live slots of a device are its first ones.
All inputs are finite; a program needn't handle non-finite values.
Results may differ from the reference program's by a relative error of at most 0.0003.
Values sent between devices are 32-bit elements; how exact they have to be, the bound alone decides.
A program may use at most 128 MiB of HBM per device.

```python
import jax
import jax.numpy as jnp
from jax import lax

CLUSTER = 512
RMAX = 96
RMIN = 32
RHS = 256
NEAR_DEV = 8
FAR_DEV = 4
DIRS = 2048
NU = 8192
N_ROW = 4
N_COL = 4
DEVICES = 32


def cluster_pairs(key, per_device):
    total = DEVICES * per_device
    slots = jnp.arange(total, dtype=jnp.int32)
    device_pos = slots // per_device
    row_group = device_pos // N_COL % N_ROW
    col_group = device_pos % N_COL
    first_key, second_key = jax.random.split(key)
    rows = row_group * N_COL + jax.random.randint(first_key, (total,), 0, N_COL, dtype=jnp.int32)
    cols = col_group * N_ROW + jax.random.randint(second_key, (total,), 0, N_ROW, dtype=jnp.int32)
    last_slot = (DEVICES - 1) * per_device
    rows = rows.at[0].set(0).at[last_slot].set(N_ROW * N_COL - 1)
    cols = cols.at[0].set(0).at[last_slot].set(N_ROW * N_COL - 1)
    return jnp.stack([rows, cols], axis=1).astype(jnp.int32)


def draw_near_pairs(key, part):
    return cluster_pairs(jax.random.fold_in(key, 11), NEAR_DEV)


def draw_far_pairs(key, part):
    return cluster_pairs(jax.random.fold_in(key, 23), FAR_DEV)


def draw_far_ranks(key, part):
    total = DEVICES * FAR_DEV
    ranks = jax.random.randint(jax.random.fold_in(key, 37), (total,), RMIN, RMAX + 1, dtype=jnp.int32)
    ranks = ranks.at[0].set(RMAX).at[FAR_DEV].set(RMIN)
    return ranks.astype(jnp.int32)


def skewed_counts(key, most):
    first_key, second_key = jax.random.split(key)
    chosen = jax.random.randint(first_key, (DEVICES,), 0, 4, dtype=jnp.int32)
    counts = jnp.where(chosen == 0, most, max(1, most // 4)).astype(jnp.int32)
    forced = jax.random.randint(second_key, (), 0, DEVICES, dtype=jnp.int32)
    return counts.at[forced].set(most)


def draw_block_counts(key, part):
    near_counts = skewed_counts(jax.random.fold_in(key, 41), NEAR_DEV)
    far_counts = skewed_counts(jax.random.fold_in(key, 43), FAR_DEV)
    return jnp.stack([near_counts, far_counts], axis=1).astype(jnp.int32)


def shard_levels(key, dims, cuts, smallest, largest):
    gain = 1.0
    for dim, shards_of in cuts:
        steps = jax.random.uniform(jax.random.fold_in(jax.random.fold_in(key, 6), dim), (shards_of,), jnp.float32, smallest / len(cuts), largest / len(cuts))
        gain = gain * jnp.repeat(jnp.exp(steps), dims[dim] // shards_of).reshape((-1,) + (1,) * (len(dims) - 1 - dim))
    return gain


def scatter_about(key, extent, spread, reach, shards=(), held_as=jnp.bfloat16):
    array = jax.random.normal(key, extent, jnp.float32) * spread
    if len(shards) > 0:
        array = shard_levels(key, extent, shards, -0.22, 0.18) * array
    return jnp.clip(array, min=-reach, max=reach).astype(held_as)


def setup_inputs(seed: int = 0) -> dict:
    streams_of = jax.random.split(jax.random.key(seed), 10)
    return {
        "cotangent": scatter_about(streams_of[0], (DIRS, 2 * RHS), 0.5, 3.0, ((0, 2),)),
        "radiation": scatter_about(streams_of[1], (2, NU, DIRS), DIRS ** -0.5, 0.125, ((1, 16), (2, 2))),
        "near_z": scatter_about(streams_of[2], (2, DEVICES * NEAR_DEV, CLUSTER, CLUSTER), CLUSTER ** -0.5, 0.25, ((1, 32),), jnp.float32),
        "near_pairs": draw_near_pairs(jax.random.fold_in(streams_of[9], 71), 0),
        "far_ut": scatter_about(streams_of[4], (2, DEVICES * FAR_DEV, RMAX, CLUSTER), CLUSTER ** -0.5, 0.25, ((1, 32),), jnp.float32),
        "far_vt": scatter_about(streams_of[5], (2, DEVICES * FAR_DEV, RMAX, CLUSTER), RMAX ** -0.5, 0.625, ((1, 32),), jnp.float32),
        "far_pairs": draw_far_pairs(jax.random.fold_in(streams_of[9], 71), 0),
        "far_ranks": draw_far_ranks(jax.random.fold_in(streams_of[9], 71), 0),
        "block_counts": draw_block_counts(jax.random.fold_in(streams_of[9], 71), 0),
    }


def swap_parts(values):
    half_width = values.shape[1] // 2
    return jnp.concatenate([-values[:, half_width:], values[:, :half_width]], axis=1)


def transposed_dot(left, right):
    return lax.dot_general(left, right, (((0,), (0,)), ((), ())), precision=lax.Precision.HIGHEST, preferred_element_type=jnp.float32)


def plain_dot(left, right):
    return jnp.dot(left, right, precision=lax.Precision.HIGHEST, preferred_element_type=jnp.float32)


def add_rows(total, term, start):
    current = lax.dynamic_slice_in_dim(total, start, term.shape[0], 0)
    return lax.dynamic_update_slice_in_dim(total, current + term, start, 0)


def reference(cotangent, radiation, near_z, near_pairs, far_ut, far_vt, far_pairs, far_ranks, block_counts):
    rhs_full = jnp.dot(radiation[0], cotangent, preferred_element_type=jnp.float32) + jnp.dot(radiation[1], swap_parts(cotangent), preferred_element_type=jnp.float32)
    rhs_swap = swap_parts(rhs_full)
    rank_most = far_ut.shape[2]

    def near_step(slot_index, total):
        slot_index = jnp.asarray(slot_index).astype(jnp.int32)
        device_pos = slot_index // NEAR_DEV
        live = (slot_index % NEAR_DEV) < block_counts[device_pos, 0]

        def apply_block(total):
            row_start = (near_pairs[slot_index, 0] * CLUSTER).astype(jnp.int32)
            col_start = (near_pairs[slot_index, 1] * CLUSTER).astype(jnp.int32)
            source = lax.dynamic_slice_in_dim(rhs_full, row_start, CLUSTER, 0)
            source_swap = lax.dynamic_slice_in_dim(rhs_swap, row_start, CLUSTER, 0)
            blocks = near_z[:, slot_index]
            term = transposed_dot(blocks[0], source) + transposed_dot(blocks[1], source_swap)
            return add_rows(total, term, col_start)

        return lax.cond(live, apply_block, lambda kept: kept, total)

    def far_step(slot_index, total):
        slot_index = jnp.asarray(slot_index).astype(jnp.int32)
        device_pos = slot_index // FAR_DEV
        live = (slot_index % FAR_DEV) < block_counts[device_pos, 1]

        def apply_block(total):
            row_start = (far_pairs[slot_index, 0] * CLUSTER).astype(jnp.int32)
            col_start = (far_pairs[slot_index, 1] * CLUSTER).astype(jnp.int32)
            source = lax.dynamic_slice_in_dim(rhs_full, row_start, CLUSTER, 0)
            source_swap = lax.dynamic_slice_in_dim(rhs_swap, row_start, CLUSTER, 0)
            left_f = far_ut[:, slot_index]
            right_f = far_vt[:, slot_index]
            coeffs = plain_dot(left_f[0], source) + plain_dot(left_f[1], source_swap)
            keep_rows = (lax.iota(jnp.int32, rank_most) < far_ranks[slot_index])[:, None]
            coeffs = jnp.where(keep_rows, coeffs, jnp.zeros_like(coeffs))
            term = transposed_dot(right_f[0], coeffs) + transposed_dot(right_f[1], swap_parts(coeffs))
            return add_rows(total, term, col_start)

        return lax.cond(live, apply_block, lambda kept: kept, total)

    total = jnp.zeros(rhs_full.shape, jnp.float32)
    total = lax.fori_loop(0, near_pairs.shape[0], near_step, total)
    total = lax.fori_loop(0, far_pairs.shape[0], far_step, total)
    return total
```

```python
import functools

import jax
import jax.numpy as jnp
from jax import lax
from jax.experimental import pallas as pl
from jax.experimental.pallas import tpu as pltpu
from jax.sharding import PartitionSpec as P

CHUNKS = 4
CORES = 2
MESH = pl.DeviceIdType.MESH
F32 = jnp.float32
BF16 = jnp.bfloat16
NT = (((1,), (1,)), ((), ()))


def dot(left, right):
    return jnp.dot(left, right, preferred_element_type=F32)


def dot_nt(left, right):
    return lax.dot_general(left, right, NT, preferred_element_type=F32)


def split(values):
    high = values.astype(BF16)
    return high, (values - high.astype(F32)).astype(BF16)


def swap_rows(values):
    half = values.shape[0] // 2
    return jnp.concatenate([-values[half:], values[:half]], axis=0)


def fold(values):
    half = values.shape[0] // 2
    return values[:half] + values[half:]


def kernel(
    n_dir, n_row, n_col, depth,
    near_pairs, far_pairs, far_ranks, counts, cot, rad, near_z, far_ut, far_vt,
    out,
    z_high, z_low, stage, ut, vt, sent, dir_in, gathered, sides, terms, parts, dir_parts, sums, row_parts,
    stage_sem, far_sem, d_send, d_recv, x_send, x_recv, c_send, c_recv, p_send, p_recv, r_send, r_recv,
):
    chunks, width = cot.shape[0], cot.shape[1]
    n_near, n_far = near_z.shape[1], far_ut.shape[1]
    block = near_z.shape[2]
    piece = block // n_dir
    n_x = n_col // CORES
    per_dir = n_row // n_dir
    d = lax.axis_index("dir")
    r = lax.axis_index("row")
    c = lax.axis_index("col")
    x, core = c // CORES, c % CORES
    partner = x * CORES + (CORES - 1 - core)

    def dir_peer(j):
        return (lax.rem(d + j, n_dir), r, c)

    def x_peer(j):
        return (d, r, lax.rem(x + j, n_x) * CORES + core)

    def row_peer(i):
        return (d, lax.rem(r + i, n_row), c)

    def from_x(j, core_of):
        return lax.rem(x + n_x - j, n_x) * CORES + core_of

    def remote(src, dst, send, recv, device):
        return pltpu.make_async_remote_copy(
            src_ref=src, dst_ref=dst, send_sem=send, recv_sem=recv, device_id=device, device_id_type=MESH
        )

    def load_item(item):
        slot, part = item // 2, lax.rem(item, 2)
        return pltpu.make_async_copy(
            near_z.at[part, slot], stage.at[lax.rem(item, 2)], stage_sem.at[lax.rem(item, 2)]
        )

    load_item(0).start()
    load_item(1).start()
    far_loads = [
        pltpu.make_async_copy(far_ut, ut, far_sem.at[0]),
        pltpu.make_async_copy(far_vt, vt, far_sem.at[1]),
    ]
    for load in far_loads:
        load.start()

    peers = [dir_peer(j) for j in range(1, n_dir)]
    peers += [x_peer(j) for j in range(1, n_x)]
    peers += [row_peer(i) for i in range(1, n_row)]
    peers.append((d, r, partner))
    barrier = pltpu.get_barrier_semaphore()
    for device in peers:
        pl.semaphore_signal(barrier, inc=1, device_id=device, device_id_type=MESH)
    pl.semaphore_wait(barrier, len(peers))

    def send_dir(k, j):
        return remote(sent.at[k], dir_in.at[k, j - 1], d_send.at[k, j - 1], d_recv.at[k, j - 1], dir_peer(j))

    def send_x(k, j):
        return remote(gathered.at[k, c], gathered.at[k, c], x_send.at[k, j - 1], x_recv.at[k, j - 1], x_peer(j))

    def send_core(k, j, core_of):
        which = from_x(j, core_of)
        return remote(
            gathered.at[k, which], gathered.at[k, which], c_send.at[k, j], c_recv.at[k, j], (d, r, partner)
        )

    def send_part(k, j, q):
        owner = lax.rem(d + j, n_dir)
        return remote(
            parts.at[k % depth, owner * n_row + q],
            dir_parts.at[k, j - 1, q],
            p_send.at[k, j - 1, q],
            p_recv.at[k, j - 1, q],
            dir_peer(j),
        )

    def send_row(k, q):
        return remote(
            sums.at[k, q], row_parts.at[k, r], r_send.at[k, q], r_recv.at[k, r], (d, q, c)
        )

    def right_sides(k):
        left = cot[k]
        sent[k] = dot_nt(left, rad[0]) + dot_nt(swap_rows(left), rad[1])
        for j in range(1, n_dir):
            send_dir(k, j).start()

    def convert(first, last):
        def body(item, carry):
            load_item(item).wait()
            high, low = split(stage[lax.rem(item, 2)])
            rows = pl.ds(pl.multiple_of(lax.rem(item, 2) * block, block), block)
            z_high[item // 2, rows, :] = high
            z_low[item // 2, rows, :] = low

            @pl.when(item + 2 < 2 * n_near)
            def _():
                load_item(item + 2).start()

            return carry

        lax.fori_loop(2 * first, 2 * last, body, 0)

    def add_dirs(k):
        for j in range(1, n_dir):
            send_dir(k, j).wait_recv()
        total = sent[k]
        for j in range(1, n_dir):
            total = total + dir_in[k, j - 1]
        gathered[k, c] = total
        for j in range(1, n_x):
            send_x(k, j).start()
        send_core(k, 0, core).start()

    def relay(k):
        for j in range(1, n_x):
            which = from_x(j, core)
            remote(
                gathered.at[k, which], gathered.at[k, which], x_send.at[k, j - 1], x_recv.at[k, j - 1], x_peer(j)
            ).wait_recv()
            send_core(k, j, core).start()

    def products(k):
        for j in range(n_x):
            send_core(k, j, CORES - 1 - core).wait_recv()

        def side(q, carry):
            values = gathered[k, q]
            high, low = split(jnp.concatenate([values, swap_rows(values)], axis=1))
            sides[q, :width] = high
            sides[q, width:] = low
            return carry

        lax.fori_loop(0, n_col, side, 0)

        def near(s, carry):
            left = sides[lax.rem(near_pairs[s, 0], n_col)]
            terms[s] = fold(dot(left, z_high[s])) + dot(left[:width], z_low[s])
            return carry

        lax.fori_loop(0, n_near, near, 0)

        def far(s, carry):
            left = sides[lax.rem(far_pairs[s, 0], n_col)]
            high, low = split(jnp.concatenate([ut[0, s], ut[1, s]], axis=1))
            coeffs = fold(dot_nt(left, high)) + dot_nt(left[:width], low)
            lanes = lax.broadcasted_iota(jnp.int32, coeffs.shape, 1)
            coeffs = jnp.where(lanes < far_ranks[s], coeffs, 0.0)
            c_high, c_low = split(coeffs)
            s_high, s_low = split(swap_rows(coeffs))
            re_high, re_low = split(vt[0, s])
            im_high, im_low = split(vt[1, s])
            both = dot(jnp.concatenate([c_high, c_low], axis=0), re_high)
            both = both + dot(jnp.concatenate([s_high, s_low], axis=0), im_high)
            terms[n_near + s] = fold(both) + (dot(c_high, re_low) + dot(s_high, im_low))
            return carry

        lax.fori_loop(0, n_far, far, 0)

        if k >= depth:
            for j in range(1, n_dir):
                for q in range(n_row):
                    send_part(k - depth, j, q).wait_send()
        for t in range(n_row):
            j, q0 = 1 + t // per_dir, (t % per_dir) * n_dir
            cluster = lax.rem(lax.rem(d + j, n_dir) * per_dir + t % per_dir, n_row)
            target = c * n_row + cluster
            gains = [
                jnp.where((near_pairs[s, 1] == target) & (s < counts[0, 0]), 1.0, 0.0) for s in range(n_near)
            ] + [
                jnp.where((far_pairs[s, 1] == target) & (s < counts[0, 1]), 1.0, 0.0) for s in range(n_far)
            ]
            for h in range(n_dir):
                lanes = slice(h * piece, (h + 1) * piece)
                total = terms[0, :, lanes] * gains[0]
                for s in range(1, n_near + n_far):
                    total = total + terms[s, :, lanes] * gains[s]
                parts[k % depth, cluster * n_dir + h] = total
                if j < n_dir:
                    send_part(k, j, q0 + h).start()
        for q in range(n_row):
            sums[k, q] = parts[k % depth, d * n_row + q]

    def add_parts(k):
        for q in range(n_row):
            for j in range(1, n_dir):
                send_part(k, j, q).wait_recv()
                sums[k, q] = sums[k, q] + dir_parts[k, j - 1, q]

            @pl.when(q != r)
            def _():
                send_row(k, q).start()

    def finish(k):
        total = sums[k, r]
        for i in range(1, n_row):
            src = lax.rem(r + i, n_row)
            remote(
                sums.at[k, src], row_parts.at[k, src], r_send.at[k, src], r_recv.at[k, src], row_peer(i)
            ).wait_recv()
            total = total + row_parts[k, src]
        out[k] = total

    for k in range(chunks):
        right_sides(k)
    steps = chunks
    edges = [n_near * i // steps for i in range(steps + 1)]
    for i in range(steps):
        convert(edges[i], edges[i + 1])
        if i < chunks - 1:
            add_dirs(i)
        if i >= 1:
            relay(i - 1)
    for load in far_loads:
        load.wait()
    products(0)
    add_dirs(chunks - 1)
    for k in range(1, chunks):
        products(k) if k < chunks - 1 else None
        if k == 1:
            relay(chunks - 1)
        if k == chunks - 1:
            add_parts(0)
            products(k)
    for k in range(1, chunks):
        add_parts(k)
        finish(k - 1)
    finish(chunks - 1)

    for k in range(chunks):
        for j in range(1, n_dir):
            send_dir(k, j).wait_send()
            if k >= chunks - depth:
                for q in range(n_row):
                    send_part(k, j, q).wait_send()
        for j in range(1, n_x):
            send_x(k, j).wait_send()
        for j in range(n_x):
            send_core(k, j, core).wait_send()
        for q in range(n_row):

            @pl.when(q != r)
            def _():
                send_row(k, q).wait_send()


def shards(
    cotangent, radiation, near_z, near_pairs, far_ut, far_vt, far_pairs, far_ranks, block_counts
):
    n_dir, n_row, n_col = (lax.axis_size(name) for name in ("dir", "row", "col"))
    deep, wide = cotangent.shape
    chunks, width = CHUNKS, wide // CHUNKS
    block = near_z.shape[2]
    n_near, n_far, rank_most = near_z.shape[1], far_ut.shape[1], far_ut.shape[2]
    n_x = n_col // CORES
    piece = block // n_dir
    depth = chunks if n_row * n_col <= 16 else 2
    cot = cotangent.T.reshape(2, chunks, width // 2, deep).transpose(1, 0, 2, 3).reshape(chunks, width, deep)
    vmem = pl.BlockSpec(memory_space=pltpu.VMEM)
    smem = pl.BlockSpec(memory_space=pltpu.SMEM)
    anywhere = pl.BlockSpec(memory_space=pl.ANY)
    dma = pltpu.SemaphoreType.DMA
    result = pl.pallas_call(
        functools.partial(kernel, n_dir, n_row, n_col, depth),
        out_shape=jax.ShapeDtypeStruct((chunks, width, piece), F32),
        in_specs=[smem] * 4 + [vmem] * 2 + [anywhere] * 3,
        out_specs=vmem,
        scratch_shapes=[
            pltpu.VMEM((n_near, 2 * block, block), BF16),
            pltpu.VMEM((n_near, 2 * block, block), BF16),
            pltpu.VMEM((2, block, block), F32),
            pltpu.VMEM(far_ut.shape, F32),
            pltpu.VMEM(far_vt.shape, F32),
            pltpu.VMEM((chunks, width, block), F32),
            pltpu.VMEM((chunks, n_dir - 1, width, block), F32),
            pltpu.VMEM((chunks, n_col, width, block), F32),
            pltpu.VMEM((n_col, 2 * width, 2 * block), BF16),
            pltpu.VMEM((n_near + n_far, width, block), F32),
            pltpu.VMEM((depth, n_dir * n_row, width, piece), F32),
            pltpu.VMEM((chunks, n_dir - 1, n_row, width, piece), F32),
            pltpu.VMEM((chunks, n_row, width, piece), F32),
            pltpu.VMEM((chunks, n_row, width, piece), F32),
            dma((2,)),
            dma((2,)),
            dma((chunks, n_dir - 1)),
            dma((chunks, n_dir - 1)),
            dma((chunks, n_x - 1)),
            dma((chunks, n_x - 1)),
            dma((chunks, n_x)),
            dma((chunks, n_x)),
            dma((chunks, n_dir - 1, n_row)),
            dma((chunks, n_dir - 1, n_row)),
            dma((chunks, n_row)),
            dma((chunks, n_row)),
        ],
        compiler_params=pltpu.CompilerParams(
            collective_id=0, has_side_effects=True, vmem_limit_bytes=67043328
        ),
    )(near_pairs, far_pairs, far_ranks, block_counts, cot, radiation, near_z, far_ut, far_vt)
    return result.reshape(chunks, 2, width // 2, piece).transpose(3, 1, 0, 2).reshape(piece, wide)


def solution(mesh):
    return jax.shard_map(
        shards,
        mesh=mesh,
        in_specs=(
            P("dir", None),
            P(None, ("row", "col"), "dir"),
            P(None, ("dir", "row", "col"), None, None),
            P(("dir", "row", "col"), None),
            P(None, ("dir", "row", "col"), None, None),
            P(None, ("dir", "row", "col"), None, None),
            P(("dir", "row", "col"), None),
            P(("dir", "row", "col")),
            P(("dir", "row", "col"), None),
        ),
        out_specs=P(("col", "dir", "row"), None),
        check_vma=False,
    )
```

```python
import functools

import jax
import jax.numpy as jnp
from jax import lax
from jax.experimental import pallas as pl
from jax.experimental.pallas import tpu as pltpu
from jax.sharding import PartitionSpec as P

CHUNKS = 4
CORES = 2
MESH = pl.DeviceIdType.MESH
F32 = jnp.float32
BF16 = jnp.bfloat16
NT = (((1,), (1,)), ((), ()))


def dot(left, right):
    return jnp.dot(left, right, preferred_element_type=F32)


def dot_nt(left, right):
    return lax.dot_general(left, right, NT, preferred_element_type=F32)


def split(values):
    high = values.astype(BF16)
    return high, (values - high.astype(F32)).astype(BF16)


def swap_rows(values):
    half = values.shape[0] // 2
    return jnp.concatenate([-values[half:], values[:half]], axis=0)


def fold(values):
    half = values.shape[0] // 2
    return values[:half] + values[half:]


def kernel(
    n_dir, n_row, n_col, depth,
    near_pairs, far_pairs, far_ranks, counts, cot, rad, near_z, far_ut, far_vt,
    out,
    z_high, z_low, stage, far_stage, left_far, right_far, cot_t, totals, sent, dir_in, gathered, sides, terms, parts, dir_parts, sums, row_parts,
    stage_sem, far_sem, d_send, d_recv, x_send, x_recv, c_send, c_recv, p_send, p_recv, r_send, r_recv,
):
    chunks, width = sent.shape[0], sent.shape[1]
    half = width // 2
    wide = cot.shape[1]
    rank_most, rank_pad = far_ut.shape[2], left_far.shape[2] // 2
    n_near, n_far = near_z.shape[1], far_ut.shape[1]
    block = near_z.shape[2]
    piece = block // n_dir
    n_x = n_col // CORES
    per_dir = n_row // n_dir
    d = lax.axis_index("dir")
    r = lax.axis_index("row")
    c = lax.axis_index("col")
    x, core = c // CORES, c % CORES
    partner = x * CORES + (CORES - 1 - core)

    def dir_peer(j):
        return (lax.rem(d + j, n_dir), r, c)

    def x_peer(j):
        return (d, r, lax.rem(x + j, n_x) * CORES + core)

    def row_peer(i):
        return (d, lax.rem(r + i, n_row), c)

    def from_x(j, core_of):
        return lax.rem(x + n_x - j, n_x) * CORES + core_of

    def remote(src, dst, send, recv, device):
        return pltpu.make_async_remote_copy(
            src_ref=src, dst_ref=dst, send_sem=send, recv_sem=recv, device_id=device, device_id_type=MESH
        )

    def load_item(item):
        slot, part = item // 2, lax.rem(item, 2)
        return pltpu.make_async_copy(
            near_z.at[part, slot], stage.at[lax.rem(item, 2)], stage_sem.at[lax.rem(item, 2)]
        )

    load_item(0).start()
    load_item(1).start()
    def load_far(s):
        side = lax.rem(s, 2)
        return [
            pltpu.make_async_copy(source.at[part, s], far_stage.at[side, 2 * i + part], far_sem.at[side, 2 * i + part])
            for i, source in enumerate((far_ut, far_vt))
            for part in range(2)
        ]

    for s in range(min(2, n_far)):
        for load in load_far(s):
            load.start()

    peers = [dir_peer(j) for j in range(1, n_dir)]
    peers += [x_peer(j) for j in range(1, n_x)]
    peers += [row_peer(i) for i in range(1, n_row)]
    peers.append((d, r, partner))
    barrier = pltpu.get_barrier_semaphore()
    for device in peers:
        pl.semaphore_signal(barrier, inc=1, device_id=device, device_id_type=MESH)
    pl.semaphore_wait(barrier, len(peers))

    def send_dir(k, j):
        return remote(sent.at[k], dir_in.at[k, j - 1], d_send.at[k, j - 1], d_recv.at[k, j - 1], dir_peer(j))

    def send_x(k, j):
        return remote(gathered.at[k, c], gathered.at[k, c], x_send.at[k, j - 1], x_recv.at[k, j - 1], x_peer(j))

    def send_core(k, j, core_of):
        which = from_x(j, core_of)
        return remote(
            gathered.at[k, which], gathered.at[k, which], c_send.at[k, j], c_recv.at[k, j], (d, r, partner)
        )

    def send_part(k, j, q):
        owner = lax.rem(d + j, n_dir)
        return remote(
            parts.at[k % depth, owner * n_row + q],
            dir_parts.at[k, j - 1, q],
            p_send.at[k, j - 1, q],
            p_recv.at[k, j - 1, q],
            dir_peer(j),
        )

    def send_row(k, q):
        return remote(
            sums.at[k, q], row_parts.at[k, r], r_send.at[k, q], r_recv.at[k, r], (d, q, c)
        )

    def right_sides(k):
        left = jnp.concatenate(
            [cot_t[k * half : (k + 1) * half], cot_t[wide // 2 + k * half : wide // 2 + (k + 1) * half]], axis=0
        )
        sent[k] = dot_nt(left, rad[0]) + dot_nt(swap_rows(left), rad[1])
        for j in range(1, n_dir):
            send_dir(k, j).start()

    def convert(first, last):
        def body(item, carry):
            load_item(item).wait()
            high, low = split(stage[lax.rem(item, 2)])
            rows = pl.ds(pl.multiple_of(lax.rem(item, 2) * block, block), block)
            z_high[item // 2, rows, :] = high
            z_low[item // 2, rows, :] = low

            @pl.when(item + 2 < 2 * n_near)
            def _():
                load_item(item + 2).start()

            return carry

        lax.fori_loop(2 * first, 2 * last, body, 0)

    def pack_far():
        rest = jnp.zeros((rank_pad - rank_most, block), F32)

        def body(s, carry):
            for load in load_far(s):
                load.wait()
            side = lax.rem(s, 2)
            for part in range(2):
                factor = jnp.concatenate([far_stage[side, part], rest], axis=0)
                high, low = split(factor.T)
                rows = slice(part * block, (part + 1) * block)
                left_far[s, rows, :rank_pad] = high
                left_far[s, rows, rank_pad:] = low
                factor = jnp.concatenate([far_stage[side, 2 + part], rest], axis=0)
                high, low = split(factor)
                rows = slice(part * rank_pad, (part + 1) * rank_pad)
                right_far[0, s, rows, :] = high
                right_far[1, s, rows, :] = low

            @pl.when(s + 2 < n_far)
            def _():
                for load in load_far(s + 2):
                    load.start()

            return carry

        lax.fori_loop(0, n_far, body, 0)

    def add_dirs(k):
        for j in range(1, n_dir):
            send_dir(k, j).wait_recv()
        total = sent[k]
        for j in range(1, n_dir):
            total = total + dir_in[k, j - 1]
        gathered[k, c] = total
        for j in range(1, n_x):
            send_x(k, j).start()
        send_core(k, 0, core).start()

    def relay(k):
        for j in range(1, n_x):
            which = from_x(j, core)
            remote(
                gathered.at[k, which], gathered.at[k, which], x_send.at[k, j - 1], x_recv.at[k, j - 1], x_peer(j)
            ).wait_recv()
            send_core(k, j, core).start()

    def products(k):
        for j in range(n_x):
            send_core(k, j, CORES - 1 - core).wait_recv()

        def side(q, carry):
            values = gathered[k, q]
            high, low = split(jnp.concatenate([values, swap_rows(values)], axis=1))
            sides[q, :width] = high
            sides[q, width:] = low
            return carry

        lax.fori_loop(0, n_col, side, 0)

        def near(s, carry):
            left = sides[lax.rem(near_pairs[s, 0], n_col)]
            terms[s] = fold(dot(left, z_high[s])) + dot(left[:width], z_low[s])
            return carry

        lax.fori_loop(0, n_near, near, 0)

        def far(s, carry):
            left = sides[lax.rem(far_pairs[s, 0], n_col)]
            both = dot(left, left_far[s])
            coeffs = fold(both[:, :rank_pad]) + both[:width, rank_pad:]
            lanes = lax.broadcasted_iota(jnp.int32, coeffs.shape, 1)
            coeffs = jnp.where(lanes < far_ranks[s], coeffs, 0.0)
            high, low = split(jnp.concatenate([coeffs, swap_rows(coeffs)], axis=1))
            both = dot(jnp.concatenate([high, low], axis=0), right_far[0, s])
            terms[n_near + s] = fold(both) + dot(high, right_far[1, s])
            return carry

        lax.fori_loop(0, n_far, far, 0)

        if k >= depth:
            for j in range(1, n_dir):
                for q in range(n_row):
                    send_part(k - depth, j, q).wait_send()
        for t in range(n_row):
            j, q0 = 1 + t // per_dir, (t % per_dir) * n_dir
            cluster = lax.rem(lax.rem(d + j, n_dir) * per_dir + t % per_dir, n_row)
            target = c * n_row + cluster
            gains = [
                jnp.where((near_pairs[s, 1] == target) & (s < counts[0, 0]), 1.0, 0.0) for s in range(n_near)
            ] + [
                jnp.where((far_pairs[s, 1] == target) & (s < counts[0, 1]), 1.0, 0.0) for s in range(n_far)
            ]
            for h in range(n_dir):
                lanes = slice(h * piece, (h + 1) * piece)
                total = terms[0, :, lanes] * gains[0]
                for s in range(1, n_near + n_far):
                    total = total + terms[s, :, lanes] * gains[s]
                parts[k % depth, cluster * n_dir + h] = total
                if j < n_dir:
                    send_part(k, j, q0 + h).start()
        for q in range(n_row):
            sums[k, q] = parts[k % depth, d * n_row + q]

    def add_parts(k):
        for q in range(n_row):
            for j in range(1, n_dir):
                send_part(k, j, q).wait_recv()
                sums[k, q] = sums[k, q] + dir_parts[k, j - 1, q]

            @pl.when(q != r)
            def _():
                send_row(k, q).start()

    def finish(k):
        total = sums[k, r]
        for i in range(1, n_row):
            src = lax.rem(r + i, n_row)
            remote(
                sums.at[k, src], row_parts.at[k, src], r_send.at[k, src], r_recv.at[k, src], row_peer(i)
            ).wait_recv()
            total = total + row_parts[k, src]
        totals[k * half : (k + 1) * half] = total[:half]
        totals[wide // 2 + k * half : wide // 2 + (k + 1) * half] = total[half:]
        if k % group == group - 1:
            for base in (0, wide // 2):
                columns = slice(base + (k + 1 - group) * half, base + (k + 1) * half)
                out[:, columns] = totals[columns].T

    group = max(1, 128 // half)
    cot_t[...] = cot[...].T
    for k in range(chunks):
        right_sides(k)
    steps = chunks
    edges = [n_near * i // steps for i in range(steps + 1)]
    for i in range(steps):
        convert(edges[i], edges[i + 1])
        if i < chunks - 1:
            add_dirs(i)
        if i >= 1:
            relay(i - 1)
    pack_far()
    products(0)
    add_dirs(chunks - 1)
    for k in range(1, chunks):
        products(k) if k < chunks - 1 else None
        if k == 1:
            relay(chunks - 1)
        if k == chunks - 1:
            add_parts(0)
            products(k)
    for k in range(1, chunks):
        add_parts(k)
        finish(k - 1)
    finish(chunks - 1)

    for k in range(chunks):
        for j in range(1, n_dir):
            send_dir(k, j).wait_send()
            if k >= chunks - depth:
                for q in range(n_row):
                    send_part(k, j, q).wait_send()
        for j in range(1, n_x):
            send_x(k, j).wait_send()
        for j in range(n_x):
            send_core(k, j, core).wait_send()
        for q in range(n_row):

            @pl.when(q != r)
            def _():
                send_row(k, q).wait_send()


def shards(
    cotangent, radiation, near_z, near_pairs, far_ut, far_vt, far_pairs, far_ranks, block_counts
):
    n_dir, n_row, n_col = (lax.axis_size(name) for name in ("dir", "row", "col"))
    deep, wide = cotangent.shape
    chunks, width = CHUNKS, wide // CHUNKS
    block = near_z.shape[2]
    n_near, n_far, rank_most = near_z.shape[1], far_ut.shape[1], far_ut.shape[2]
    n_x = n_col // CORES
    piece = block // n_dir
    depth = chunks if n_row * n_col <= 16 else 2
    rank_pad = -(-rank_most // 128) * 128
    vmem = pl.BlockSpec(memory_space=pltpu.VMEM)
    smem = pl.BlockSpec(memory_space=pltpu.SMEM)
    anywhere = pl.BlockSpec(memory_space=pl.ANY)
    dma = pltpu.SemaphoreType.DMA
    return pl.pallas_call(
        functools.partial(kernel, n_dir, n_row, n_col, depth),
        out_shape=jax.ShapeDtypeStruct((piece, wide), F32),
        in_specs=[smem] * 4 + [vmem] * 2 + [anywhere] * 3,
        out_specs=vmem,
        scratch_shapes=[
            pltpu.VMEM((n_near, 2 * block, block), BF16),
            pltpu.VMEM((n_near, 2 * block, block), BF16),
            pltpu.VMEM((2, block, block), F32),
            pltpu.VMEM((2, 4, rank_most, block), F32),
            pltpu.VMEM((n_far, 2 * block, 2 * rank_pad), BF16),
            pltpu.VMEM((2, n_far, 2 * rank_pad, block), BF16),
            pltpu.VMEM((wide, deep), BF16),
            pltpu.VMEM((wide, piece), F32),
            pltpu.VMEM((chunks, width, block), F32),
            pltpu.VMEM((chunks, n_dir - 1, width, block), F32),
            pltpu.VMEM((chunks, n_col, width, block), F32),
            pltpu.VMEM((n_col, 2 * width, 2 * block), BF16),
            pltpu.VMEM((n_near + n_far, width, block), F32),
            pltpu.VMEM((depth, n_dir * n_row, width, piece), F32),
            pltpu.VMEM((chunks, n_dir - 1, n_row, width, piece), F32),
            pltpu.VMEM((chunks, n_row, width, piece), F32),
            pltpu.VMEM((chunks, n_row, width, piece), F32),
            dma((2,)),
            dma((2, 4)),
            dma((chunks, n_dir - 1)),
            dma((chunks, n_dir - 1)),
            dma((chunks, n_x - 1)),
            dma((chunks, n_x - 1)),
            dma((chunks, n_x)),
            dma((chunks, n_x)),
            dma((chunks, n_dir - 1, n_row)),
            dma((chunks, n_dir - 1, n_row)),
            dma((chunks, n_row)),
            dma((chunks, n_row)),
        ],
        compiler_params=pltpu.CompilerParams(
            collective_id=0, has_side_effects=True, vmem_limit_bytes=67043328
        ),
    )(near_pairs, far_pairs, far_ranks, block_counts, cotangent, radiation, near_z, far_ut, far_vt)


def solution(mesh):
    return jax.shard_map(
        shards,
        mesh=mesh,
        in_specs=(
            P("dir", None),
            P(None, ("row", "col"), "dir"),
            P(None, ("dir", "row", "col"), None, None),
            P(("dir", "row", "col"), None),
            P(None, ("dir", "row", "col"), None, None),
            P(None, ("dir", "row", "col"), None, None),
            P(("dir", "row", "col"), None),
            P(("dir", "row", "col")),
            P(("dir", "row", "col"), None),
        ),
        out_specs=P(("col", "dir", "row"), None),
        check_vma=False,
    )
```

```python
import functools

import jax
import jax.numpy as jnp
from jax import lax
from jax.experimental import pallas as pl
from jax.experimental.pallas import tpu as pltpu
from jax.sharding import PartitionSpec as P

CHUNKS = 4
CORES = 2
MESH = pl.DeviceIdType.MESH
F32 = jnp.float32
BF16 = jnp.bfloat16
NT = (((1,), (1,)), ((), ()))


def dot(left, right):
    return jnp.dot(left, right, preferred_element_type=F32)


def dot_nt(left, right):
    return lax.dot_general(left, right, NT, preferred_element_type=F32)


def split(values):
    high = values.astype(BF16)
    return high, (values - high.astype(F32)).astype(BF16)


def swap_rows(values):
    half = values.shape[0] // 2
    return jnp.concatenate([-values[half:], values[:half]], axis=0)


def fold(values):
    half = values.shape[0] // 2
    return values[:half] + values[half:]


def kernel(
    n_dir, n_row, n_col, depth,
    near_pairs, far_pairs, far_ranks, counts, cot, rad, near_z, far_ut, far_vt,
    out,
    z_high, z_low, stage, far_stage, left_far, right_far, cot_t, totals, sent, dir_in, gathered, sides, terms, parts, dir_parts, sums, row_parts,
    stage_sem, far_sem, d_send, d_recv, x_send, x_recv, c_send, c_recv, p_send, p_recv, r_send, r_recv,
):
    chunks, width = sent.shape[0], sent.shape[1]
    half = width // 2
    wide = cot.shape[1]
    stages = stage.shape[0]
    rank_most, rank_pad = far_ut.shape[2], left_far.shape[2] // 2
    n_near, n_far = near_z.shape[1], far_ut.shape[1]
    block = near_z.shape[2]
    piece = block // n_dir
    n_x = n_col // CORES
    per_dir = n_row // n_dir
    d = lax.axis_index("dir")
    r = lax.axis_index("row")
    c = lax.axis_index("col")
    x, core = c // CORES, c % CORES
    partner = x * CORES + (CORES - 1 - core)

    def dir_peer(j):
        return (lax.rem(d + j, n_dir), r, c)

    def x_peer(j):
        return (d, r, lax.rem(x + j, n_x) * CORES + core)

    def row_peer(i):
        return (d, lax.rem(r + i, n_row), c)

    def from_x(j, core_of):
        return lax.rem(x + n_x - j, n_x) * CORES + core_of

    def remote(src, dst, send, recv, device):
        return pltpu.make_async_remote_copy(
            src_ref=src, dst_ref=dst, send_sem=send, recv_sem=recv, device_id=device, device_id_type=MESH
        )

    def load_item(item):
        slot, part = item // 2, lax.rem(item, 2)
        return pltpu.make_async_copy(
            near_z.at[part, slot], stage.at[lax.rem(item, stages)], stage_sem.at[lax.rem(item, stages)]
        )

    for item in range(stages):
        load_item(item).start()
    def load_far(s):
        side = lax.rem(s, 2)
        return [
            pltpu.make_async_copy(source.at[part, s], far_stage.at[side, 2 * i + part], far_sem.at[side, 2 * i + part])
            for i, source in enumerate((far_ut, far_vt))
            for part in range(2)
        ]

    for s in range(min(2, n_far)):
        for load in load_far(s):
            load.start()

    peers = [dir_peer(j) for j in range(1, n_dir)]
    peers += [x_peer(j) for j in range(1, n_x)]
    peers += [row_peer(i) for i in range(1, n_row)]
    peers.append((d, r, partner))
    barrier = pltpu.get_barrier_semaphore()
    for device in peers:
        pl.semaphore_signal(barrier, inc=1, device_id=device, device_id_type=MESH)
    pl.semaphore_wait(barrier, len(peers))

    def send_dir(k, j):
        return remote(sent.at[k], dir_in.at[k, j - 1], d_send.at[k, j - 1], d_recv.at[k, j - 1], dir_peer(j))

    def send_x(k, j):
        return remote(gathered.at[k, c], gathered.at[k, c], x_send.at[k, j - 1], x_recv.at[k, j - 1], x_peer(j))

    def send_core(k, j, core_of):
        which = from_x(j, core_of)
        return remote(
            gathered.at[k, which], gathered.at[k, which], c_send.at[k, j], c_recv.at[k, j], (d, r, partner)
        )

    def send_part(k, j, q):
        owner = lax.rem(d + j, n_dir)
        return remote(
            parts.at[k % depth, owner * n_row + q],
            dir_parts.at[k, j - 1, q],
            p_send.at[k, j - 1, q],
            p_recv.at[k, j - 1, q],
            dir_peer(j),
        )

    def send_row(k, q):
        return remote(
            sums.at[k, q], row_parts.at[k, r], r_send.at[k, q], r_recv.at[k, r], (d, q, c)
        )

    def right_sides(k):
        left = jnp.concatenate(
            [cot_t[k * half : (k + 1) * half], cot_t[wide // 2 + k * half : wide // 2 + (k + 1) * half]], axis=0
        )
        sent[k] = dot_nt(left, rad[0]) + dot_nt(swap_rows(left), rad[1])
        for j in range(1, n_dir):
            send_dir(k, j).start()

    def convert(first, last):
        def body(item, carry):
            load_item(item).wait()
            high, low = split(stage[lax.rem(item, stages)])
            rows = pl.ds(pl.multiple_of(lax.rem(item, 2) * block, block), block)
            z_high[item // 2, rows, :] = high
            z_low[item // 2, rows, :] = low

            @pl.when(item + stages < 2 * n_near)
            def _():
                load_item(item + stages).start()

            return carry

        lax.fori_loop(2 * first, 2 * last, body, 0)

    def pack_far():
        rest = jnp.zeros((rank_pad - rank_most, block), F32)

        def body(s, carry):
            for load in load_far(s):
                load.wait()
            side = lax.rem(s, 2)
            for part in range(2):
                factor = jnp.concatenate([far_stage[side, part], rest], axis=0)
                high, low = split(factor.T)
                rows = slice(part * block, (part + 1) * block)
                left_far[s, rows, :rank_pad] = high
                left_far[s, rows, rank_pad:] = low
                factor = jnp.concatenate([far_stage[side, 2 + part], rest], axis=0)
                high, low = split(factor)
                rows = slice(part * rank_pad, (part + 1) * rank_pad)
                right_far[0, s, rows, :] = high
                right_far[1, s, rows, :] = low

            @pl.when(s + 2 < n_far)
            def _():
                for load in load_far(s + 2):
                    load.start()

            return carry

        lax.fori_loop(0, n_far, body, 0)

    def add_dirs(k):
        for j in range(1, n_dir):
            send_dir(k, j).wait_recv()
        total = sent[k]
        for j in range(1, n_dir):
            total = total + dir_in[k, j - 1]
        gathered[k, c] = total
        for j in range(1, n_x):
            send_x(k, j).start()
        send_core(k, 0, core).start()

    def relay(k):
        for j in range(1, n_x):
            which = from_x(j, core)
            remote(
                gathered.at[k, which], gathered.at[k, which], x_send.at[k, j - 1], x_recv.at[k, j - 1], x_peer(j)
            ).wait_recv()
            send_core(k, j, core).start()

    def products(k):
        for j in range(n_x):
            send_core(k, j, CORES - 1 - core).wait_recv()

        def side(q, carry):
            values = gathered[k, q]
            high, low = split(jnp.concatenate([values, swap_rows(values)], axis=1))
            sides[q, :width] = high
            sides[q, width:] = low
            return carry

        lax.fori_loop(0, n_col, side, 0)

        per_far = n_near // n_far

        def near(s):
            left = sides[lax.rem(near_pairs[s, 0], n_col)]
            terms[s] = fold(dot(left, z_high[s])) + dot(left[:width], z_low[s])

        def body(s, carry):
            both = dot(sides[lax.rem(far_pairs[s, 0], n_col)], left_far[s])
            near(s * per_far)
            coeffs = fold(both[:, :rank_pad]) + both[:width, rank_pad:]
            lanes = lax.broadcasted_iota(jnp.int32, coeffs.shape, 1)
            coeffs = jnp.where(lanes < far_ranks[s], coeffs, 0.0)
            high, low = split(jnp.concatenate([coeffs, swap_rows(coeffs)], axis=1))
            for i in range(1, per_far):
                near(s * per_far + i)
            both = dot(jnp.concatenate([high, low], axis=0), right_far[0, s])
            terms[n_near + s] = fold(both) + dot(high, right_far[1, s])
            return carry

        lax.fori_loop(0, n_far, body, 0)

        if k >= depth:
            for j in range(1, n_dir):
                for q in range(n_row):
                    send_part(k - depth, j, q).wait_send()
        for t in range(n_row):
            j, q0 = 1 + t // per_dir, (t % per_dir) * n_dir
            cluster = lax.rem(lax.rem(d + j, n_dir) * per_dir + t % per_dir, n_row)
            target = c * n_row + cluster
            gains = [
                jnp.where((near_pairs[s, 1] == target) & (s < counts[0, 0]), 1.0, 0.0) for s in range(n_near)
            ] + [
                jnp.where((far_pairs[s, 1] == target) & (s < counts[0, 1]), 1.0, 0.0) for s in range(n_far)
            ]
            for h in range(n_dir):
                lanes = slice(h * piece, (h + 1) * piece)
                total = terms[0, :, lanes] * gains[0]
                for s in range(1, n_near + n_far):
                    total = total + terms[s, :, lanes] * gains[s]
                parts[k % depth, cluster * n_dir + h] = total
                if j < n_dir:
                    send_part(k, j, q0 + h).start()
        for q in range(n_row):
            sums[k, q] = parts[k % depth, d * n_row + q]

    def add_parts(k):
        for q in range(n_row):
            for j in range(1, n_dir):
                send_part(k, j, q).wait_recv()
                sums[k, q] = sums[k, q] + dir_parts[k, j - 1, q]

            @pl.when(q != r)
            def _():
                send_row(k, q).start()

    def finish(k):
        total = sums[k, r]
        for i in range(1, n_row):
            src = lax.rem(r + i, n_row)
            remote(
                sums.at[k, src], row_parts.at[k, src], r_send.at[k, src], r_recv.at[k, src], row_peer(i)
            ).wait_recv()
            total = total + row_parts[k, src]
        totals[k * half : (k + 1) * half] = total[:half]
        totals[wide // 2 + k * half : wide // 2 + (k + 1) * half] = total[half:]
        if k % group == group - 1:
            for base in (0, wide // 2):
                columns = slice(base + (k + 1 - group) * half, base + (k + 1) * half)
                out[:, columns] = totals[columns].T

    group = max(1, 128 // half)
    cot_t[...] = cot[...].T
    for k in range(chunks):
        right_sides(k)
    steps = chunks
    edges = [n_near * i // steps for i in range(steps + 1)]
    for i in range(steps):
        convert(edges[i], edges[i + 1])
        if i < chunks - 1:
            add_dirs(i)
        if i >= 1:
            relay(i - 1)
    pack_far()
    products(0)
    add_dirs(chunks - 1)
    for k in range(1, chunks):
        products(k) if k < chunks - 1 else None
        if k == 1:
            relay(chunks - 1)
        if k == chunks - 1:
            add_parts(0)
            products(k)
    for k in range(1, chunks):
        add_parts(k)
        finish(k - 1)
    finish(chunks - 1)

    for k in range(chunks):
        for j in range(1, n_dir):
            send_dir(k, j).wait_send()
            if k >= chunks - depth:
                for q in range(n_row):
                    send_part(k, j, q).wait_send()
        for j in range(1, n_x):
            send_x(k, j).wait_send()
        for j in range(n_x):
            send_core(k, j, core).wait_send()
        for q in range(n_row):

            @pl.when(q != r)
            def _():
                send_row(k, q).wait_send()


def shards(
    cotangent, radiation, near_z, near_pairs, far_ut, far_vt, far_pairs, far_ranks, block_counts
):
    n_dir, n_row, n_col = (lax.axis_size(name) for name in ("dir", "row", "col"))
    deep, wide = cotangent.shape
    chunks, width = CHUNKS, wide // CHUNKS
    block = near_z.shape[2]
    n_near, n_far, rank_most = near_z.shape[1], far_ut.shape[1], far_ut.shape[2]
    n_x = n_col // CORES
    piece = block // n_dir
    small = n_row * n_col <= 16
    depth = chunks if small else 2
    stages = min(6 if small else 2, 2 * n_near)
    rank_pad = -(-rank_most // 128) * 128
    vmem = pl.BlockSpec(memory_space=pltpu.VMEM)
    smem = pl.BlockSpec(memory_space=pltpu.SMEM)
    anywhere = pl.BlockSpec(memory_space=pl.ANY)
    dma = pltpu.SemaphoreType.DMA
    return pl.pallas_call(
        functools.partial(kernel, n_dir, n_row, n_col, depth),
        out_shape=jax.ShapeDtypeStruct((piece, wide), F32),
        in_specs=[smem] * 4 + [vmem] * 2 + [anywhere] * 3,
        out_specs=vmem,
        scratch_shapes=[
            pltpu.VMEM((n_near, 2 * block, block), BF16),
            pltpu.VMEM((n_near, 2 * block, block), BF16),
            pltpu.VMEM((stages, block, block), F32),
            pltpu.VMEM((2, 4, rank_most, block), F32),
            pltpu.VMEM((n_far, 2 * block, 2 * rank_pad), BF16),
            pltpu.VMEM((2, n_far, 2 * rank_pad, block), BF16),
            pltpu.VMEM((wide, deep), BF16),
            pltpu.VMEM((wide, piece), F32),
            pltpu.VMEM((chunks, width, block), F32),
            pltpu.VMEM((chunks, n_dir - 1, width, block), F32),
            pltpu.VMEM((chunks, n_col, width, block), F32),
            pltpu.VMEM((n_col, 2 * width, 2 * block), BF16),
            pltpu.VMEM((n_near + n_far, width, block), F32),
            pltpu.VMEM((depth, n_dir * n_row, width, piece), F32),
            pltpu.VMEM((chunks, n_dir - 1, n_row, width, piece), F32),
            pltpu.VMEM((chunks, n_row, width, piece), F32),
            pltpu.VMEM((chunks, n_row, width, piece), F32),
            dma((stages,)),
            dma((2, 4)),
            dma((chunks, n_dir - 1)),
            dma((chunks, n_dir - 1)),
            dma((chunks, n_x - 1)),
            dma((chunks, n_x - 1)),
            dma((chunks, n_x)),
            dma((chunks, n_x)),
            dma((chunks, n_dir - 1, n_row)),
            dma((chunks, n_dir - 1, n_row)),
            dma((chunks, n_row)),
            dma((chunks, n_row)),
        ],
        compiler_params=pltpu.CompilerParams(
            collective_id=0, has_side_effects=True, vmem_limit_bytes=67043328
        ),
    )(near_pairs, far_pairs, far_ranks, block_counts, cotangent, radiation, near_z, far_ut, far_vt)


def solution(mesh):
    return jax.shard_map(
        shards,
        mesh=mesh,
        in_specs=(
            P("dir", None),
            P(None, ("row", "col"), "dir"),
            P(None, ("dir", "row", "col"), None, None),
            P(("dir", "row", "col"), None),
            P(None, ("dir", "row", "col"), None, None),
            P(None, ("dir", "row", "col"), None, None),
            P(("dir", "row", "col"), None),
            P(("dir", "row", "col")),
            P(("dir", "row", "col"), None),
        ),
        out_specs=P(("col", "dir", "row"), None),
        check_vma=False,
    )
```
